128 devices in a mesh: req: 16 (over y, z), mdl: 8 (over x, core).
Axes of the slice: x: 4, y: 4, z: 4, core: 2. Of those that a mesh axis runs over, the one named last changes fastest.
Arguments:
- segments: int32 [1024], P('req'), may hold values from -1 to 1023, as said below
- queries: bfloat16 [1024, 8192], P('req', 'mdl'), may hold values from -200 to 200
- keys_values: bfloat16 [1024, 2, 1024], P('req', None, 'mdl'), may hold values from -6 to 6
- page_table: int32 [64], replicated, may hold values from 0 to 127, as said below
- paged_cache: bfloat16 [128, 16, 2, 1024], P('req', None, None, 'mdl'), may hold values from -6 to 6
- residual: bfloat16 [1024, 8192], P(None, 'req'), may hold values from -40 to 40
- out_weight: bfloat16 [8192, 8192], P('mdl', 'req'), may hold values from -0.0625 to 0.0625
- norm_gain: bfloat16 [8192], P('req'), may hold values from 0.099609375 to 1.8984375
- gate_up_weight: bfloat16 [8192, 2, 29568], P('req', None, 'mdl'), may hold values from -0.0625 to 0.0625
Outputs:
- hidden: bfloat16 [1024, 29568], P('req', 'mdl')
- cache_new: bfloat16 [128, 16, 2, 1024], P('req', None, None, 'mdl')
The draws below stay inside these ranges and needn't reach their ends.
Inputs may be any that keep to these rules, and one draw needn't show every extreme that they name: `segments`: each block of 64 slots of one index of req holds whole requests followed by pads; a live slot's entry is the slot index of its request's first slot, in that block; in every draw some block has no pads. `page_table`: all entries differ; page p lies on index p // 8 of req; the pages of one block of 64 slots all lie on one index of req, and different blocks on different indices.
All inputs are finite; a program needn't handle non-finite values.
Results may differ from the reference program's by a relative error of at most 0.024.
Values may be sent and summed in bfloat16 or wider, within the bound.
A program may use at most 128 MiB of HBM per device.

```python
import jax
import jax.numpy as jnp
from jax import lax

D = 8192
FF = 29568
HQ = 64
KVH = 8
HD = 128
QPK = 8
TOK_DEV = 64
TOKENS = 1024
PAGE = 16
CPD = 8
N_REQ = 16


def segment_starts(key):
    blocks = TOKENS // TOK_DEV
    full_key, live_key, rate_key, bits_key = jax.random.split(key, 4)
    full_block = jax.random.randint(full_key, (), 0, blocks)
    lives = jax.random.randint(live_key, (blocks,), TOK_DEV // 4, TOK_DEV + 1)
    lives = jnp.where(jnp.arange(blocks) == full_block, TOK_DEV, lives)
    choices_rate = jax.random.randint(rate_key, (blocks,), 0, 3)
    rates = jnp.where(choices_rate == 0, 4, jnp.where(choices_rate == 1, 16, 64))
    draws = jax.random.randint(bits_key, (blocks, TOK_DEV), 0, 1 << 20)
    place = jnp.arange(TOK_DEV)[None, :]
    starts = (draws % rates[:, None] == 0) | (place == 0)
    begin = lax.cummax(jnp.where(starts, place, 0), axis=1)
    anchor = jnp.arange(blocks)[:, None] * TOK_DEV
    result = jnp.where(place < lives[:, None], anchor + begin, -1)
    return result.reshape(TOKENS).astype(jnp.int32)


def queries_and_pairs(key):
    query_key, key_key, value_key = jax.random.split(jax.random.fold_in(key, 23), 3)
    keys = jnp.clip(jax.random.normal(key_key, (TOKENS, KVH, HD)), -6.0, 6.0)
    query = jnp.clip(jax.random.normal(query_key, (TOKENS, KVH, HQ // KVH, HD)), -6.0, 6.0)
    values = jnp.clip(jax.random.normal(value_key, (TOKENS, KVH, HD)), -6.0, 6.0)
    pairs = jnp.stack([keys.reshape(TOKENS, KVH * HD), values.reshape(TOKENS, KVH * HD)], axis=1)
    return (query.reshape(TOKENS, HQ * HD), pairs)


def draw_segments(key, part):
    return segment_starts(jax.random.fold_in(key, 11))


def draw_queries(key, part):
    return queries_and_pairs(key)[0].astype(jnp.bfloat16)


def draw_keys_values(key, part):
    return queries_and_pairs(key)[1].astype(jnp.bfloat16)


def draw_page_table(key, part):
    blocks = N_REQ
    per_block = TOK_DEV // PAGE
    owner_key, shift_key, order_key = jax.random.split(jax.random.fold_in(key, 31), 3)
    owners = jax.random.permutation(owner_key, blocks).astype(jnp.int32)
    shifts = jax.random.randint(shift_key, (blocks,), 0, CPD).astype(jnp.int32)
    shifts = jnp.where(owners == 0, 0, jnp.where(owners == blocks - 1, CPD - per_block, shifts)).astype(jnp.int32)
    local = (shifts[:, None] + jnp.arange(per_block, dtype=jnp.int32)[None, :]) % CPD
    row_keys = jax.random.split(order_key, blocks)
    local = jax.vmap(lambda row_key, row: jax.random.permutation(row_key, row))(row_keys, local)
    pages = owners[:, None] * CPD + local
    return pages.reshape(blocks * per_block).astype(jnp.int32)


def draw_residual(key, part):
    base_key, column_key, row_key = jax.random.split(jax.random.fold_in(key, 41), 3)
    trend = jnp.exp(jnp.linspace(jnp.log(0.7), jnp.log(1.2), D))
    column = trend * jnp.exp(jax.random.uniform(column_key, (D,), minval=-0.55, maxval=0.55))
    row = jnp.exp(jax.random.uniform(row_key, (TOKENS,), minval=jnp.log(0.4), maxval=jnp.log(4.0)))
    base = jax.random.normal(base_key, (TOKENS, D))
    return jnp.clip(base * row[:, None] * column[None, :], -40.0, 40.0).astype(jnp.bfloat16)


def block_levels(stream_key, extent, cuts, low, top_value):
    def one(dim, blocks):
        steps = jax.random.uniform(jax.random.fold_in(jax.random.fold_in(stream_key, 6), dim), (blocks,), jnp.float32, low / len(cuts), top_value / len(cuts))
        return jnp.repeat(jnp.exp(steps), extent[dim] // blocks).reshape((-1,) + (1,) * (len(extent) - dim - 1))

    loudness = one(*cuts[0])
    for cut in cuts[1:]:
        loudness = loudness * one(*cut)
    return loudness


def normal_values(key, shape, spread, most, cuts=(), kind=jnp.bfloat16):
    array = jax.random.normal(key, shape, jnp.float32) * spread
    if len(cuts) > 0:
        array = block_levels(key, shape, cuts, -0.22, 0.18) * array
    return jnp.clip(array, min=-most, max=most).astype(kind)


def setup_inputs(seed: int = 0) -> dict:
    arg_keys = jax.random.split(jax.random.key(seed), 10)
    return {
        "segments": draw_segments(jax.random.fold_in(arg_keys[9], 71), 0),
        "queries": draw_queries(jax.random.fold_in(arg_keys[9], 71), 0),
        "keys_values": draw_keys_values(jax.random.fold_in(arg_keys[9], 71), 0),
        "page_table": draw_page_table(jax.random.fold_in(arg_keys[9], 71), 0),
        "paged_cache": normal_values(arg_keys[4], (N_REQ * CPD, PAGE, 2, KVH * HD), 1.0, 6.0, ((0, 16), (3, 8))),
        "residual": draw_residual(jax.random.fold_in(arg_keys[9], 71), 0),
        "out_weight": normal_values(arg_keys[6], (HQ * HD, D), (HQ * HD) ** -0.5, 0.0625, ((0, 8), (1, 16))),
        "norm_gain": jnp.clip(1.0 + 0.18 * jax.random.normal(arg_keys[7], (D,), jnp.float32), 0.099609375, 1.8984375).astype(jnp.bfloat16),
        "gate_up_weight": normal_values(arg_keys[8], (D, 2, FF), D ** -0.5, 0.0625, ((0, 16), (2, 8))),
    }


EPSILON = 1e-06

def attention_block(query_rows, pair_rows, seg_rows):
    slots = seg_rows.shape[0]
    groups = pair_rows.shape[2] // HD
    query = query_rows.reshape(slots, groups, QPK, HD).astype(jnp.float32)
    keys = pair_rows[:, 0].reshape(slots, groups, HD).astype(jnp.float32)
    values = pair_rows[:, 1].reshape(slots, groups, HD).astype(jnp.float32)
    scores = jnp.einsum('igqd,jgd->gqij', query, keys) * HD ** (-0.5)
    places = jnp.arange(slots, dtype=jnp.int32)
    allowed = (seg_rows[:, None] == seg_rows[None, :]) & (seg_rows[:, None] >= 0) & (places[None, :] < places[:, None])
    allowed = allowed | (places[:, None] == places[None, :])
    scores = jnp.where(allowed, scores, -jnp.inf)
    highest = lax.optimization_barrier(jnp.max(scores, axis=-1, keepdims=True))
    weights = jnp.exp(scores - highest)
    probs = (weights / lax.optimization_barrier(jnp.sum(weights, axis=-1, keepdims=True))).astype(jnp.bfloat16)
    mixed = jnp.einsum('gqij,jgd->igqd', probs.astype(jnp.float32), values)
    mixed = jnp.where((seg_rows >= 0)[:, None, None, None], mixed, 0.0)
    return mixed.reshape(slots, groups * QPK * HD).astype(jnp.bfloat16)

def reference(segments, queries, keys_values, page_table, paged_cache, residual, out_weight, norm_gain, gate_up_weight):
    attended = jax.vmap(attention_block)(queries.reshape(N_REQ, TOK_DEV, HQ * HD), keys_values.reshape(N_REQ, TOK_DEV, 2, KVH * HD), segments.reshape(N_REQ, TOK_DEV)).reshape(TOKENS, HQ * HD)
    stream = residual.astype(jnp.float32) + jnp.dot(attended, out_weight, preferred_element_type=jnp.float32)
    totals = lax.optimization_barrier(jnp.sum(stream * stream, axis=1))
    normed = (stream * lax.rsqrt(totals / D + EPSILON)[:, None] * norm_gain.astype(jnp.float32)[None, :]).astype(jnp.bfloat16)
    width = D // N_REQ
    flat_weight = gate_up_weight.reshape(D, 2 * FF)

    def add_group(running, group):
        start = (group * width).astype(jnp.int32)
        rows_in = lax.dynamic_slice_in_dim(normed, start, width, 1)
        weight_rows = lax.dynamic_slice_in_dim(flat_weight, start, width, 0)
        part = jnp.dot(rows_in, weight_rows, preferred_element_type=jnp.float32).astype(jnp.bfloat16)
        part = lax.optimization_barrier(part)
        return (running + part.astype(jnp.float32), None)
    summed, _ = lax.scan(add_group, jnp.zeros((TOKENS, 2 * FF), jnp.float32), jnp.arange(N_REQ, dtype=jnp.int32))
    hidden = (jax.nn.silu(summed[:, :FF]) * summed[:, FF:]).astype(jnp.bfloat16)
    pages = jnp.repeat(page_table, PAGE, total_repeat_length=TOKENS)
    target = jnp.where(segments >= 0, pages, N_REQ * CPD).astype(jnp.int32)
    offsets = (jnp.arange(TOKENS, dtype=jnp.int32) % PAGE).astype(jnp.int32)
    cache_new = paged_cache.at[target, offsets].set(keys_values, mode='drop')
    return (hidden, cache_new)
```

```python
import functools

import jax
import jax.numpy as jnp
from jax import lax
from jax.experimental import pallas as pl
from jax.experimental.pallas import tpu as pltpu
from jax.sharding import PartitionSpec as P

D = 8192
HD = 128
QPK = 8
PAGE = 16
EPSILON = 1e-06
MESH = pl.DeviceIdType.MESH
F32 = jnp.float32
BF16 = jnp.bfloat16
DEAD = 512.0
NT = (((1,), (1,)), ((), ()))


def position():
    req, mdl = lax.axis_index("req"), lax.axis_index("mdl")
    return req // 4, req % 4, mdl // 2, mdl % 2


def dev(y, z, x, c):
    return (y * 4 + z, x * 2 + c)


def ring(v, step):
    return lax.rem(v + step + 4, 4)


def barrier(peers):
    sem = pltpu.get_barrier_semaphore()
    for peer in peers:
        pl.semaphore_signal(sem, inc=1, device_id=peer, device_id_type=MESH)
    pl.semaphore_wait(sem, len(peers))


def copy_to(src, dst, ssem, rsem, peer):
    return pltpu.make_async_remote_copy(
        src_ref=src, dst_ref=dst, send_sem=ssem, recv_sem=rsem, device_id=peer, device_id_type=MESH
    )


def front_kernel(
    q_ref, k_ref, v_ref, segc_ref, segr_ref, pages_ref, cache_ref, res_ref, ow_ref, gain_ref,
    ng_ref, cout_ref,
    ag, acc_own, p2s, p2r, s2s, s2r, chunk_own, n2,
    ag_ss, ag_rs, p_ss, p_rs, x_ss, x_rs, n_ss, n_rs,
):
    y, z, x, c = position()
    me = (y, z, x, c)
    zp, zm = dev(y, ring(z, 1), x, c), dev(y, ring(z, -1), x, c)
    yp, ym = dev(ring(y, 1), z, x, c), dev(ring(y, -1), z, x, c)
    xp, xm = dev(y, z, ring(x, 1), c), dev(y, z, ring(x, -1), c)
    partner = dev(y, z, x, 1 - c)
    barrier((zp, zm, yp, ym, xp, xm, partner))
    started = []

    def go(copy):
        copy.start()
        started.append(copy)
        return copy

    segc, segr = segc_ref[...], segr_ref[...]
    row = lax.broadcasted_iota(jnp.int32, (64, 64), 0)
    col = lax.broadcasted_iota(jnp.int32, (64, 64), 1)
    allowed = ((segc == segr) & (segc >= 0) & (col < row)) | (col == row)
    live = segc >= 0
    keys, values = k_ref[...], v_ref[...]
    for h in range(QPK):
        s = lax.dot_general(q_ref[:, h * HD : (h + 1) * HD], keys, NT, preferred_element_type=F32)
        s = jnp.where(allowed, s * HD ** (-0.5), -jnp.inf)
        w = jnp.exp(s - jnp.max(s, axis=-1, keepdims=True))
        probs = (w / jnp.sum(w, axis=-1, keepdims=True)).astype(BF16)
        mixed = jnp.dot(probs, values, preferred_element_type=F32)
        half, at = h // 4, (h % 4) * HD
        ag[half, y, z, :, at : at + HD] = jnp.where(live, mixed, 0.0).astype(BF16)
    ag[0, y, z, :, 512:640] = jnp.where(live, keys.astype(F32), DEAD).astype(BF16)
    ag[1, y, z, :, 512:640] = jnp.where(live, values.astype(F32), DEAD).astype(BF16)

    first = ((zp, zm), (yp, ym))
    second = ((yp, ym), (zp, zm))

    def spot(half, f, s):
        return (s, f) if half == 0 else (f, s)

    fc, sc = (z, y), (y, z)

    def block(half, f, s, lo=0, n=64):
        a, b = spot(half, f, s)
        return ag.at[half, a, b, pl.ds(lo, n)]

    def ag_copy(half, j, k, ref, peer):
        return copy_to(ref, ref, ag_ss.at[half, j, k], ag_rs.at[half, j, k], peer)

    one = [[None] * 4 for _ in range(2)]
    two = [[[None] * 4 for _ in range(4)] for _ in range(2)]
    offs = (0, -1, 1, 2)

    def start_one(half):
        ref = block(half, fc[half], sc[half])
        for k in range(2):
            one[half][k] = go(ag_copy(half, 4, k, ref, first[half][k]))

    def forward_one(half, k):
        one[half][k].wait_recv()
        ref = block(half, ring(fc[half], -1 if k == 0 else 1), sc[half], 32 * k, 32)
        one[half][2 + k] = go(ag_copy(half, 4, 2 + k, ref, first[half][k]))

    def start_two(half, j):
        ref = block(half, ring(fc[half], offs[j]), sc[half])
        for k in range(2):
            two[half][j][k] = go(ag_copy(half, j, k, ref, second[half][k]))

    def forward_two(half, j):
        for k in range(2):
            two[half][j][k].wait_recv()
            ref = block(half, ring(fc[half], offs[j]), ring(sc[half], -1 if k == 0 else 1), 32 * k, 32)
            two[half][j][2 + k] = go(ag_copy(half, j, 2 + k, ref, second[half][k]))

    def finish_one(half):
        for k in (2, 3):
            one[half][k].wait_recv()

    def finish_two(half, j):
        for k in (2, 3):
            two[half][j][k].wait_recv()

    p_copy = [None] * 4

    def project(g):
        ya = ring(y, offs[g])
        acc = jnp.dot(ag[0, ya, :, :, :512].reshape(256, 512), ow_ref[:512], preferred_element_type=F32)
        acc += jnp.dot(ag[1, ya, :, :, :512].reshape(256, 512), ow_ref[512:], preferred_element_type=F32)
        low, high = acc[:, :256], acc[:, 256:]
        acc_own[g] = jnp.where(c == 0, low, high)
        p2s[g] = jnp.where(c == 0, high, low).astype(BF16)
        p_copy[g] = go(copy_to(p2s.at[g], p2r.at[g], p_ss.at[g], p_rs.at[g], partner))

    for half in range(2):
        start_one(half)
    for half in range(2):
        start_two(half, 0)
    for half in range(2):
        for k in range(2):
            forward_one(half, k)
            start_two(half, 1 + k)
    for half in range(2):
        forward_two(half, 0)
    for half in range(2):
        finish_one(half)
        start_two(half, 3)
    finish_two(1, 0)
    project(0)
    for half in range(2):
        for j in (1, 2):
            forward_two(half, j)
    for half in range(2):
        forward_two(half, 3)
    finish_two(1, 1)
    project(1)
    finish_two(1, 2)
    project(2)
    finish_two(1, 3)
    for j in range(4):
        finish_two(0, j)
    project(3)

    x_copy = [[None] * 10 for _ in range(4)]
    n_copy = [None] * 4
    top, bot = slice(0, 32), slice(32, 64)

    def xmsg(g, i, k, rows, peer):
        return go(copy_to(s2s.at[g, k, rows], s2r.at[g, k, rows], x_ss.at[g, i], x_rs.at[g, i], peer))

    ds_top, ds_bot = pl.ds(0, 32), pl.ds(32, 32)
    for g in range(4):
        p_copy[g].wait_recv()

        def part(xx):
            rows = pl.ds(pl.multiple_of(xx * 64, 64), 64)
            return acc_own[g, rows, :] + p2r[g, rows, :].astype(F32)

        s2s[g, 0] = part(ring(x, 2)).astype(BF16)
        x_copy[g][0] = xmsg(g, 0, 0, ds_top, xp)
        x_copy[g][1] = xmsg(g, 1, 0, ds_bot, xm)
        s2s[g, 1] = part(ring(x, 1)).astype(BF16)
        x_copy[g][2] = xmsg(g, 2, 1, ds_bot, xp)
        s2s[g, 2] = part(ring(x, -1)).astype(BF16)
        x_copy[g][3] = xmsg(g, 3, 2, ds_top, xm)
        chunk_own[g] = part(x)
    for g in range(4):
        x_copy[g][0].wait_recv()
        s2s[g, 1, top] = (s2s[g, 1, top].astype(F32) + s2r[g, 0, top].astype(F32)).astype(BF16)
        x_copy[g][4] = xmsg(g, 4, 1, ds_top, xp)
        x_copy[g][1].wait_recv()
        s2s[g, 2, bot] = (s2s[g, 2, bot].astype(F32) + s2r[g, 0, bot].astype(F32)).astype(BF16)
        x_copy[g][5] = xmsg(g, 5, 2, ds_bot, xm)

    def nmsg(g, i, ref, peer):
        return go(copy_to(ref, ref, x_ss.at[g, i], x_rs.at[g, i], peer))

    gain = jnp.where(c == 0, gain_ref[:, :256], gain_ref[:, 256:])
    for g in range(4):
        ya = ring(y, offs[g])
        for i in (2, 3, 4, 5):
            x_copy[g][i].wait_recv()
        total = chunk_own[g] + s2r[g, 1].astype(F32) + s2r[g, 2].astype(F32)
        res = res_ref[ya, x].astype(F32)
        stream = total + jnp.where(c == 0, res[:, :256], res[:, 256:])
        n2[ya, c, x] = (stream * gain).astype(BF16)
        ref = n2.at[ya, c, x]
        x_copy[g][6] = nmsg(g, 6, ref, xp)
        x_copy[g][7] = nmsg(g, 7, ref, xm)
    for g in range(4):
        ya = ring(y, offs[g])
        x_copy[g][6].wait_recv()
        x_copy[g][8] = nmsg(g, 8, n2.at[ya, c, ring(x, -1), ds_top], xp)
        x_copy[g][7].wait_recv()
        x_copy[g][9] = nmsg(g, 9, n2.at[ya, c, ring(x, 1), ds_bot], xm)
    for g in range(4):
        ya = ring(y, offs[g])
        x_copy[g][8].wait_recv()
        x_copy[g][9].wait_recv()
        ref = n2.at[ya, c]
        n_copy[g] = go(copy_to(ref, ref, n_ss.at[g], n_rs.at[g], partner))

    req = lax.axis_index("req")
    base = req * 8
    slot = lax.broadcasted_iota(jnp.int32, (128, 1024), 0)
    tok = lax.broadcasted_iota(jnp.int32, (128, 1024), 1)
    hit = (pages_ref[...] == base + slot // PAGE) & (slot % PAGE == tok % PAGE)
    pick = jnp.where(hit, 1.0, 0.0)
    has = jnp.sum(pick, axis=1, keepdims=True) > 0.5
    pick = pick.astype(BF16)
    for half in range(2):
        new = jnp.dot(pick, ag[half, :, :, :, 512:640].reshape(1024, 128), preferred_element_type=F32)
        old = cache_ref[:, half * 128 : half * 128 + 128]
        cout_ref[:, half * 128 : half * 128 + 128] = jnp.where(
            has & (new < 0.5 * DEAD), new, old.astype(F32)
        ).astype(BF16)

    for g in range(4):
        ya = ring(y, offs[g])
        n_copy[g].wait_recv()
        for h in range(2):
            ng_ref[ya, :, :, h * 256 : h * 256 + 256] = n2[ya, h]
    for copy in started:
        copy.wait_send()


def front(q, k, v, segc, segr, pages, cache, res, ow, gain):
    vm = pl.BlockSpec(memory_space=pltpu.VMEM)
    dma = pltpu.SemaphoreType.DMA
    return pl.pallas_call(
        front_kernel,
        out_shape=(
            jax.ShapeDtypeStruct((4, 4, 64, 512), BF16),
            jax.ShapeDtypeStruct((128, 256), BF16),
        ),
        in_specs=[vm] * 10,
        out_specs=(vm, vm),
        scratch_shapes=[
            pltpu.VMEM((2, 4, 4, 64, 640), BF16),
            pltpu.VMEM((4, 256, 256), F32),
            pltpu.VMEM((4, 256, 256), BF16),
            pltpu.VMEM((4, 256, 256), BF16),
            pltpu.VMEM((4, 3, 64, 256), BF16),
            pltpu.VMEM((4, 3, 64, 256), BF16),
            pltpu.VMEM((4, 64, 256), F32),
            pltpu.VMEM((4, 2, 4, 64, 256), BF16),
            dma((2, 5, 4)), dma((2, 5, 4)),
            dma((4,)), dma((4,)),
            dma((4, 10)), dma((4, 10)),
            dma((4,)), dma((4,)),
        ],
        compiler_params=pltpu.CompilerParams(collective_id=0, has_side_effects=True, vmem_limit_bytes=60 << 20),
        name="front",
    )(q, k, v, segc, segr, pages, cache, res, ow, gain)


WIDE = 3712
COLS = 3696
PIECES = ((2688, 1024), (0, 896), (896, 896), (1792, 896))


def back_kernel(
    ng_ref, ginv_ref, w_ref, out_ref,
    w, ss, own1, own2, rscale, s1, r1, s2, r2,
    w_sem, ss1, rs1, ss2, rs2,
):
    y, z, x, c = position()
    zp, zm = dev(y, ring(z, 1), x, c), dev(y, ring(z, -1), x, c)
    yp, ym = dev(ring(y, 1), z, x, c), dev(ring(y, -1), z, x, c)
    loads = []
    for p, (lo, n) in enumerate(PIECES):
        for g in range(2):
            m = min(n, COLS - lo)
            loads.append(
                pltpu.make_async_copy(w_ref.at[g, pl.ds(lo, m)], w.at[g, pl.ds(lo, m)], w_sem.at[p, g])
            )
            loads[-1].start()
    barrier((zp, zm, yp, ym))
    started = []

    def go(copy):
        copy.start()
        started.append(copy)
        return copy

    first = ((zp, zm), (yp, ym))
    second = ((yp, ym), (zp, zm))
    fc, sc = (z, y), (y, z)
    r = lax.axis_index("req")
    ginv = ginv_ref[...]
    for a in range(4):
        v = ng_ref[a].reshape(256, 512).astype(F32) * ginv
        ss[a] = jnp.broadcast_to(jnp.sum(v * v, axis=1, keepdims=True), (256, 128)).reshape(4, 64, 128)

    def rows_of(ref, g, d, n):
        v = ref[:, pl.ds(d, 1)] if g == 0 else ref[pl.ds(d, 1)]
        return v.reshape(256, n)

    def partial(g, d, p):
        lo, n = PIECES[p]
        out = lax.dot_general(rows_of(ng_ref, g, d, 512), w[g, lo : lo + n], NT, preferred_element_type=F32)
        if lo + n > COLS:
            tot = rows_of(ss, g, d, 128)
            high = tot.astype(BF16).astype(F32)
            mine = high if g == 0 else tot - high
            lane = lax.broadcasted_iota(jnp.int32, (256, 128), 1)
            tail = out[:, n - 128 :]
            tail = jnp.where(lane < 112, tail, jnp.where(lane == 112 + r, mine, 0.0))
            out = jnp.concatenate([out[:, : n - 128], tail], axis=1)
        return out.reshape(4, 64, n)

    one = [[[None] * 6 for _ in range(2)] for _ in range(4)]
    two = [[[None] * 6 for _ in range(2)] for _ in range(4)]

    def send1(p, g, i, k, t, peer):
        lo, n = PIECES[p]
        at = (g, k, pl.ds(t, 2), slice(None), pl.ds(lo, n))
        one[p][g][i] = go(copy_to(s1.at[at], r1.at[at], ss1.at[p, g, i], rs1.at[p, g, i], peer))

    def send2(p, g, i, k, t, peer):
        lo, n = PIECES[p]
        at = (g, k, pl.ds(t, 32), pl.ds(lo, n))
        two[p][g][i] = go(copy_to(s2.at[at], r2.at[at], ss2.at[p, g, i], rs2.at[p, g, i], peer))

    def stage_x(p):
        lo, n = PIECES[p]
        hi = lo + n
        for g in range(2):
            loads[2 * p + g].wait()
            s1[g, 0, :, :, lo:hi] = partial(g, ring(fc[g], 2), p).astype(BF16)
            send1(p, g, 0, 0, 0, first[g][0])
            send1(p, g, 1, 0, 2, first[g][1])
        for g in range(2):
            s1[g, 1, :, :, lo:hi] = partial(g, ring(fc[g], 1), p).astype(BF16)
            send1(p, g, 2, 1, 2, first[g][0])
            s1[g, 2, :, :, lo:hi] = partial(g, ring(fc[g], -1), p).astype(BF16)
            send1(p, g, 3, 2, 0, first[g][1])

    def stage_y(p):
        lo, n = PIECES[p]
        hi = lo + n
        for g in range(2):
            for k in range(2):
                t = 2 * k
                one[p][g][k].wait_recv()
                v = s1[g, 1 + k, t : t + 2, :, lo:hi].astype(F32) + r1[g, 0, t : t + 2, :, lo:hi].astype(F32)
                s1[g, 1 + k, t : t + 2, :, lo:hi] = v.astype(BF16)
                send1(p, g, 4 + k, 1 + k, t, first[g][k])

    def stage_z(p):
        lo, n = PIECES[p]
        hi = lo + n
        for g in range(2):
            own1[g, :, :, :n] = partial(g, fc[g], p)
        for g in range(2):
            for i in (2, 3, 4, 5):
                one[p][g][i].wait_recv()

            def summed(t):
                at = (pl.ds(t, 1), slice(None))
                return (
                    own1[g, pl.ds(t, 1), :, :n]
                    + r1[g, 1, pl.ds(t, 1), :, lo:hi].astype(F32)
                    + r1[g, 2, pl.ds(t, 1), :, lo:hi].astype(F32)
                ).reshape(64, n)

            s2[g, 0, :, lo:hi] = summed(ring(sc[g], 2)).astype(BF16)
            send2(p, g, 0, 0, 0, second[g][0])
            send2(p, g, 1, 0, 32, second[g][1])
            s2[g, 1, :, lo:hi] = summed(ring(sc[g], 1)).astype(BF16)
            send2(p, g, 2, 1, 32, second[g][0])
            s2[g, 2, :, lo:hi] = summed(ring(sc[g], -1)).astype(BF16)
            send2(p, g, 3, 2, 0, second[g][1])
            own2[g, :, lo:hi] = summed(sc[g])

    def stage_u(p):
        lo, n = PIECES[p]
        hi = lo + n
        for g in range(2):
            for k in range(2):
                t = 32 * k
                two[p][g][k].wait_recv()
                v = s2[g, 1 + k, t : t + 32, lo:hi].astype(F32) + r2[g, 0, t : t + 32, lo:hi].astype(F32)
                s2[g, 1 + k, t : t + 32, lo:hi] = v.astype(BF16)
                send2(p, g, 4 + k, 1 + k, t, second[g][k])

    def stage_v(p):
        lo, n = PIECES[p]
        hi = lo + n
        val = []
        for g in range(2):
            for i in (2, 3, 4, 5):
                two[p][g][i].wait_recv()
            val.append(own2[g, :, lo:hi] + r2[g, 1, :, lo:hi].astype(F32) + r2[g, 2, :, lo:hi].astype(F32))
        if hi > COLS:
            lane = lax.broadcasted_iota(jnp.int32, (64, 128), 1)
            tail = val[0][:, n - 128 :] + val[1][:, n - 128 :]
            tot = jnp.sum(jnp.where(lane >= 112, tail, 0.0), axis=1, keepdims=True)
            rscale[...] = jnp.broadcast_to(lax.rsqrt(tot / D + EPSILON), (64, 128))
        scale = rscale[:, :1]
        gate, up = val[0] * scale, val[1] * scale
        hidden = (gate / (1.0 + jnp.exp(-gate)) * up).astype(BF16)
        m = min(n, COLS - lo)
        out_ref[:, lo : lo + m] = hidden[:, :m]

    for stage, p in (
        (stage_x, 0), (stage_x, 1), (stage_y, 0), (stage_x, 2), (stage_y, 1), (stage_z, 0),
        (stage_x, 3), (stage_y, 2), (stage_z, 1), (stage_u, 0), (stage_y, 3), (stage_z, 2),
        (stage_u, 1), (stage_v, 0), (stage_z, 3), (stage_u, 2), (stage_v, 1), (stage_u, 3),
        (stage_v, 2), (stage_v, 3),
    ):
        stage(p)
    for copy in started:
        copy.wait_send()


def back(ng, ginv, wt):
    vm = pl.BlockSpec(memory_space=pltpu.VMEM)
    dma = pltpu.SemaphoreType.DMA
    return pl.pallas_call(
        back_kernel,
        out_shape=jax.ShapeDtypeStruct((64, COLS), BF16),
        in_specs=[vm, vm, pl.BlockSpec(memory_space=pl.ANY)],
        out_specs=vm,
        scratch_shapes=[
            pltpu.VMEM((2, WIDE, 512), BF16),
            pltpu.VMEM((4, 4, 64, 128), F32),
            pltpu.VMEM((2, 4, 64, 1024), F32),
            pltpu.VMEM((2, 64, WIDE), F32),
            pltpu.VMEM((64, 128), F32),
            pltpu.VMEM((2, 3, 4, 64, WIDE), BF16),
            pltpu.VMEM((2, 3, 4, 64, WIDE), BF16),
            pltpu.VMEM((2, 3, 64, WIDE), BF16),
            pltpu.VMEM((2, 3, 64, WIDE), BF16),
            dma((4, 2)),
            dma((4, 2, 6)), dma((4, 2, 6)),
            dma((4, 2, 6)), dma((4, 2, 6)),
        ],
        compiler_params=pltpu.CompilerParams(collective_id=1, has_side_effects=True, vmem_limit_bytes=67043328),
        name="back",
    )(ng, ginv, wt)


def on_device(
    segments, queries, keys_values, page_table, paged_cache, residual, out_weight, norm_gain, gate_up_weight
):
    keys, values = keys_values[:, 0], keys_values[:, 1]
    pages = jnp.broadcast_to(page_table[:, None], (64, PAGE)).reshape(1, 1024)
    gain = norm_gain.astype(F32)[None, :]
    ng, cache = front(
        queries, keys, values, segments[:, None], segments[None, :], pages,
        paged_cache.reshape(128, 256), residual.reshape(4, 4, 64, 512), out_weight, gain,
    )
    wt = gate_up_weight.transpose(1, 2, 0)
    hidden = back(ng, 1.0 / gain, wt)
    return hidden, cache.reshape(8, 16, 2, 128)


def solution(mesh):
    placed = (
        P("req"),
        P("req", "mdl"),
        P("req", None, "mdl"),
        P(),
        P("req", None, None, "mdl"),
        P(None, "req"),
        P("mdl", "req"),
        P("req"),
        P("req", None, "mdl"),
    )
    return jax.shard_map(
        on_device,
        mesh=mesh,
        in_specs=placed,
        out_specs=(P("req", "mdl"), P("req", None, None, "mdl")),
        check_vma=False,
    )
```

```python
import jax
import jax.numpy as jnp
from jax import lax
from jax.experimental import pallas as pl
from jax.experimental.pallas import tpu as pltpu
from jax.sharding import PartitionSpec as P

D = 8192
HD = 128
QPK = 8
PAGE = 16
EPSILON = 1e-06
MESH = pl.DeviceIdType.MESH
F32 = jnp.float32
BF16 = jnp.bfloat16
DEAD = 512.0
NT = (((1,), (1,)), ((), ()))


def position():
    req, mdl = lax.axis_index("req"), lax.axis_index("mdl")
    return req // 4, req % 4, mdl // 2, mdl % 2


def dev(y, z, x, c):
    return (y * 4 + z, x * 2 + c)


def ring(v, step):
    return lax.rem(v + step + 4, 4)


def barrier(peers):
    sem = pltpu.get_barrier_semaphore()
    for peer in peers:
        pl.semaphore_signal(sem, inc=1, device_id=peer, device_id_type=MESH)
    pl.semaphore_wait(sem, len(peers))


def copy_to(src, dst, ssem, rsem, peer):
    return pltpu.make_async_remote_copy(
        src_ref=src, dst_ref=dst, send_sem=ssem, recv_sem=rsem, device_id=peer, device_id_type=MESH
    )


WIDE = 3712
COLS = 3696
PIECES = ((2688, 1024), (0, 896), (896, 896), (1792, 896))


def layer_kernel(
    seg_ref, pages_ref, gain_ref, q_ref, kv_ref, cache_ref, res_hbm, ow_hbm, w_ref,
    out_ref, cout_ref,
    res_ref, ow_ref, ag, kvb, acc_own, p2s, p2r, s2s, s2r, chunk_own, n2, ng_ref,
    w, ss, own1, own2, rscale, s1, r1, s2, r2,
    in_sem, w_sem, ag_ss, ag_rs, kv_ss, kv_rs, p_ss, p_rs, x_ss, x_rs, n_ss, n_rs,
    ss1, rs1, ss2, rs2,
):
    y, z, x, c = position()
    zp, zm = dev(y, ring(z, 1), x, c), dev(y, ring(z, -1), x, c)
    yp, ym = dev(ring(y, 1), z, x, c), dev(ring(y, -1), z, x, c)
    xp, xm = dev(y, z, ring(x, 1), c), dev(y, z, ring(x, -1), c)
    partner = dev(y, z, x, 1 - c)
    ow_load = pltpu.make_async_copy(ow_hbm, ow_ref, in_sem.at[0])
    res_load = pltpu.make_async_copy(res_hbm, res_ref, in_sem.at[1])
    ow_load.start()
    res_load.start()
    loads = []
    for p, (lo, n) in enumerate(PIECES):
        for g in range(2):
            m = min(n, COLS - lo)
            loads.append(
                pltpu.make_async_copy(w_ref.at[g, pl.ds(lo, m)], w.at[g, pl.ds(lo, m)], w_sem.at[p, g])
            )
            loads[-1].start()
    started = []

    def go(copy):
        copy.start()
        started.append(copy)
        return copy

    seg = jnp.broadcast_to(seg_ref[...].astype(F32), (128, 64))
    wide_row = lax.broadcasted_iota(jnp.int32, (128, 64), 0)
    wide_col = lax.broadcasted_iota(jnp.int32, (128, 64), 1)
    seg_kv = jnp.sum(jnp.where(wide_col == wide_row // 2, seg, 0.0), axis=1, keepdims=True)
    segc = jnp.sum(jnp.where(wide_col == wide_row, seg, 0.0)[:64], axis=1, keepdims=True)
    row = lax.broadcasted_iota(jnp.int32, (64, 128), 0)
    col = lax.broadcasted_iota(jnp.int32, (64, 128), 1)
    segr = jnp.sum(jnp.where(col // 2 == row, segc, 0.0), axis=0, keepdims=True)
    allowed = ((segc == segr) & (segc >= 0) & (col // 2 < row)) | (col // 2 == row)
    allowed = allowed & (col % 2 == 0)
    live = segc >= 0
    kv = kv_ref[...]
    for h in range(QPK):
        s = lax.dot_general(q_ref[:, h * HD : (h + 1) * HD], kv, NT, preferred_element_type=F32)
        s = jnp.where(allowed, s * HD ** (-0.5), -jnp.inf)
        e = jnp.exp(s - jnp.max(s, axis=-1, keepdims=True))
        probs = pltpu.roll(e / jnp.sum(e, axis=-1, keepdims=True), 1, 1).astype(BF16)
        mixed = jnp.dot(probs, kv, preferred_element_type=F32)
        half, at = h // 4, (h % 4) * HD
        ag[half, y, z, :, at : at + HD] = jnp.where(live, mixed, 0.0).astype(BF16)
    kvb[y, z] = jnp.where(seg_kv >= 0, kv.astype(F32), DEAD).astype(BF16)
    barrier((zp, zm, yp, ym, xp, xm, partner))

    first = ((zp, zm), (yp, ym))
    second = ((yp, ym), (zp, zm))
    fc, sc = (z, y), (y, z)

    def block(half, f, s, lo=0, n=64):
        a, b = (s, f) if half == 0 else (f, s)
        return ag.at[half, a, b, pl.ds(lo, n)]

    def ag_copy(half, j, k, ref, peer):
        return copy_to(ref, ref, ag_ss.at[half, j, k], ag_rs.at[half, j, k], peer)

    one = [[None] * 4 for _ in range(2)]
    two = [[[None] * 4 for _ in range(4)] for _ in range(2)]
    offs = (0, -1, 1, 2)

    def start_one(half):
        ref = block(half, fc[half], sc[half])
        for k in range(2):
            one[half][k] = go(ag_copy(half, 4, k, ref, first[half][k]))

    def forward_one(half, k):
        one[half][k].wait_recv()
        ref = block(half, ring(fc[half], -1 if k == 0 else 1), sc[half], 32 * k, 32)
        one[half][2 + k] = go(ag_copy(half, 4, 2 + k, ref, first[half][k]))

    def start_two(half, j):
        ref = block(half, ring(fc[half], offs[j]), sc[half])
        for k in range(2):
            two[half][j][k] = go(ag_copy(half, j, k, ref, second[half][k]))

    def forward_two(half, j):
        for k in range(2):
            two[half][j][k].wait_recv()
            ref = block(half, ring(fc[half], offs[j]), ring(sc[half], -1 if k == 0 else 1), 32 * k, 32)
            two[half][j][2 + k] = go(ag_copy(half, j, 2 + k, ref, second[half][k]))

    def finish_one(half):
        for k in (2, 3):
            one[half][k].wait_recv()

    def finish_two(half, j):
        for k in (2, 3):
            two[half][j][k].wait_recv()

    kv_copy = [None] * 8

    def kv_msg(i, ref, peer):
        kv_copy[i] = go(copy_to(ref, ref, kv_ss.at[i], kv_rs.at[i], peer))

    def kv_start():
        kv_msg(0, kvb.at[y, z], zp)
        kv_msg(1, kvb.at[y, z], zm)

    def kv_forward():
        kv_copy[0].wait_recv()
        kv_msg(2, kvb.at[y, ring(z, -1), pl.ds(0, 64)], zp)
        kv_copy[1].wait_recv()
        kv_msg(3, kvb.at[y, ring(z, 1), pl.ds(64, 64)], zm)

    def kv_rows():
        kv_copy[2].wait_recv()
        kv_copy[3].wait_recv()
        kv_msg(4, kvb.at[y], yp)
        kv_msg(5, kvb.at[y], ym)

    def kv_rows_forward():
        kv_copy[4].wait_recv()
        kv_msg(6, kvb.at[ring(y, -1), pl.ds(0, 2)], yp)
        kv_copy[5].wait_recv()
        kv_msg(7, kvb.at[ring(y, 1), pl.ds(2, 2)], ym)

    p_copy = [None] * 4
    x_copy = [[None] * 10 for _ in range(4)]
    n_copy = [None] * 4
    top, bot = slice(0, 32), slice(32, 64)
    ds_top, ds_bot = pl.ds(0, 32), pl.ds(32, 32)

    def project(g):
        ya = ring(y, offs[g])
        acc = jnp.dot(ag[0, ya].reshape(256, 512), ow_ref[:512], preferred_element_type=F32)
        acc += jnp.dot(ag[1, ya].reshape(256, 512), ow_ref[512:], preferred_element_type=F32)
        low, high = acc[:, :256], acc[:, 256:]
        acc_own[g] = jnp.where(c == 0, low, high)
        p2s[g] = jnp.where(c == 0, high, low).astype(BF16)
        p_copy[g] = go(copy_to(p2s.at[g], p2r.at[g], p_ss.at[g], p_rs.at[g], partner))

    def xmsg(g, i, k, rows, peer):
        x_copy[g][i] = go(copy_to(s2s.at[g, k, rows], s2r.at[g, k, rows], x_ss.at[g, i], x_rs.at[g, i], peer))

    def reduce_a(g):
        p_copy[g].wait_recv()

        def part(xx):
            rows = pl.ds(pl.multiple_of(xx * 64, 64), 64)
            return acc_own[g, rows, :] + p2r[g, rows, :].astype(F32)

        s2s[g, 0] = part(ring(x, 2)).astype(BF16)
        xmsg(g, 0, 0, ds_top, xp)
        xmsg(g, 1, 0, ds_bot, xm)
        s2s[g, 1] = part(ring(x, 1)).astype(BF16)
        xmsg(g, 2, 1, ds_bot, xp)
        s2s[g, 2] = part(ring(x, -1)).astype(BF16)
        xmsg(g, 3, 2, ds_top, xm)
        chunk_own[g] = part(x)

    def reduce_b(g):
        x_copy[g][0].wait_recv()
        s2s[g, 1, top] = (s2s[g, 1, top].astype(F32) + s2r[g, 0, top].astype(F32)).astype(BF16)
        xmsg(g, 4, 1, ds_top, xp)
        x_copy[g][1].wait_recv()
        s2s[g, 2, bot] = (s2s[g, 2, bot].astype(F32) + s2r[g, 0, bot].astype(F32)).astype(BF16)
        xmsg(g, 5, 2, ds_bot, xm)

    def nmsg(g, i, ref, peer):
        x_copy[g][i] = go(copy_to(ref, ref, x_ss.at[g, i], x_rs.at[g, i], peer))

    gain_row = gain_ref[...].astype(F32)
    gain = jnp.where(c == 0, gain_row[:, :256], gain_row[:, 256:])
    ginv = 1.0 / gain_row

    def reduce_c(g):
        ya = ring(y, offs[g])
        for i in (2, 3, 4, 5):
            x_copy[g][i].wait_recv()
        total = chunk_own[g] + s2r[g, 1].astype(F32) + s2r[g, 2].astype(F32)
        res = res_ref[ya, x].astype(F32)
        stream = total + jnp.where(c == 0, res[:, :256], res[:, 256:])
        n2[ya, c, x] = (stream * gain).astype(BF16)
        nmsg(g, 6, n2.at[ya, c, x], xp)
        nmsg(g, 7, n2.at[ya, c, x], xm)

    def reduce_d(g):
        ya = ring(y, offs[g])
        x_copy[g][6].wait_recv()
        nmsg(g, 8, n2.at[ya, c, ring(x, -1), ds_top], xp)
        x_copy[g][7].wait_recv()
        nmsg(g, 9, n2.at[ya, c, ring(x, 1), ds_bot], xm)

    def reduce_e(g):
        ya = ring(y, offs[g])
        x_copy[g][8].wait_recv()
        x_copy[g][9].wait_recv()
        ref = n2.at[ya, c]
        n_copy[g] = go(copy_to(ref, ref, n_ss.at[g], n_rs.at[g], partner))

    def reduce_f(g):
        ya = ring(y, offs[g])
        n_copy[g].wait_recv()
        squares = 0.0
        for h in range(2):
            at = slice(h * 256, h * 256 + 256)
            v = n2[ya, h]
            ng_ref[ya, :, :, at] = v
            v = v.reshape(256, 256).astype(F32) * ginv[:, at]
            squares += jnp.sum(v * v, axis=1, keepdims=True)
        ss[ya] = jnp.broadcast_to(squares, (256, 128)).reshape(4, 64, 128)

    for half in range(2):
        start_one(half)
    for half in range(2):
        start_two(half, 0)
    for half in range(2):
        for k in range(2):
            forward_one(half, k)
            start_two(half, 1 + k)
    for half in range(2):
        forward_two(half, 0)
    for half in range(2):
        finish_one(half)
        start_two(half, 3)
    kv_start()
    ow_load.wait()
    finish_two(1, 0)
    project(0)
    for j in (1, 2):
        for half in range(2):
            forward_two(half, j)
    reduce_a(0)
    for half in range(2):
        forward_two(half, 3)
    finish_two(1, 1)
    project(1)
    reduce_b(0)
    finish_two(1, 2)
    project(2)
    kv_forward()
    reduce_a(1)
    res_load.wait()
    reduce_c(0)
    reduce_a(2)
    reduce_b(1)
    finish_two(1, 3)
    for j in range(4):
        finish_two(0, j)
    project(3)
    kv_rows()
    reduce_d(0)
    reduce_b(2)
    reduce_c(1)
    reduce_a(3)
    reduce_e(0)
    reduce_d(1)
    reduce_c(2)
    reduce_b(3)
    reduce_e(1)
    reduce_f(0)
    reduce_d(2)
    reduce_c(3)
    reduce_e(2)
    reduce_f(1)
    kv_rows_forward()
    reduce_d(3)
    reduce_f(2)
    reduce_e(3)
    reduce_f(3)

    r = lax.axis_index("req")

    def rows_of(ref, g, d, n):
        v = ref[:, pl.ds(d, 1)] if g == 0 else ref[pl.ds(d, 1)]
        return v.reshape(256, n)

    def partial(g, d, p):
        lo, n = PIECES[p]
        out = lax.dot_general(rows_of(ng_ref, g, d, 512), w[g, lo : lo + n], NT, preferred_element_type=F32)
        if lo + n > COLS:
            tot = rows_of(ss, g, d, 128)
            high = tot.astype(BF16).astype(F32)
            mine = high if g == 0 else tot - high
            lane = lax.broadcasted_iota(jnp.int32, (256, 128), 1)
            tail = out[:, n - 128 :]
            tail = jnp.where(lane < 112, tail, jnp.where(lane == 112 + r, mine, 0.0))
            out = jnp.concatenate([out[:, : n - 128], tail], axis=1)
        return out.reshape(4, 64, n)

    fast = [[[None] * 6 for _ in range(2)] for _ in range(4)]
    slow = [[[None] * 6 for _ in range(2)] for _ in range(4)]

    def send1(p, g, i, k, t, peer):
        lo, n = PIECES[p]
        at = (g, k, pl.ds(t, 2), slice(None), pl.ds(lo, n))
        fast[p][g][i] = go(copy_to(s1.at[at], r1.at[at], ss1.at[p, g, i], rs1.at[p, g, i], peer))

    def send2(p, g, i, k, t, peer):
        lo, n = PIECES[p]
        at = (g, k, pl.ds(t, 32), pl.ds(lo, n))
        slow[p][g][i] = go(copy_to(s2.at[at], r2.at[at], ss2.at[p, g, i], rs2.at[p, g, i], peer))

    def stage_x(p):
        lo, n = PIECES[p]
        hi = lo + n
        for g in range(2):
            loads[2 * p + g].wait()
            s1[g, 0, :, :, lo:hi] = partial(g, ring(fc[g], 2), p).astype(BF16)
            send1(p, g, 0, 0, 0, first[g][0])
            send1(p, g, 1, 0, 2, first[g][1])
        for g in range(2):
            s1[g, 1, :, :, lo:hi] = partial(g, ring(fc[g], 1), p).astype(BF16)
            send1(p, g, 2, 1, 2, first[g][0])
            s1[g, 2, :, :, lo:hi] = partial(g, ring(fc[g], -1), p).astype(BF16)
            send1(p, g, 3, 2, 0, first[g][1])

    def stage_y(p):
        lo, n = PIECES[p]
        hi = lo + n
        for g in range(2):
            for k in range(2):
                t = 2 * k
                fast[p][g][k].wait_recv()
                v = s1[g, 1 + k, t : t + 2, :, lo:hi].astype(F32) + r1[g, 0, t : t + 2, :, lo:hi].astype(F32)
                s1[g, 1 + k, t : t + 2, :, lo:hi] = v.astype(BF16)
                send1(p, g, 4 + k, 1 + k, t, first[g][k])

    def stage_z(p):
        lo, n = PIECES[p]
        hi = lo + n
        for g in range(2):
            own1[g, :, :, :n] = partial(g, fc[g], p)
        for g in range(2):
            for i in (2, 3, 4, 5):
                fast[p][g][i].wait_recv()

            def summed(t):
                at = (pl.ds(t, 1), slice(None))
                return (
                    own1[g, pl.ds(t, 1), :, :n]
                    + r1[g, 1, pl.ds(t, 1), :, lo:hi].astype(F32)
                    + r1[g, 2, pl.ds(t, 1), :, lo:hi].astype(F32)
                ).reshape(64, n)

            s2[g, 0, :, lo:hi] = summed(ring(sc[g], 2)).astype(BF16)
            send2(p, g, 0, 0, 0, second[g][0])
            send2(p, g, 1, 0, 32, second[g][1])
            s2[g, 1, :, lo:hi] = summed(ring(sc[g], 1)).astype(BF16)
            send2(p, g, 2, 1, 32, second[g][0])
            s2[g, 2, :, lo:hi] = summed(ring(sc[g], -1)).astype(BF16)
            send2(p, g, 3, 2, 0, second[g][1])
            own2[g, :, lo:hi] = summed(sc[g])

    def stage_u(p):
        lo, n = PIECES[p]
        hi = lo + n
        for g in range(2):
            for k in range(2):
                t = 32 * k
                slow[p][g][k].wait_recv()
                v = s2[g, 1 + k, t : t + 32, lo:hi].astype(F32) + r2[g, 0, t : t + 32, lo:hi].astype(F32)
                s2[g, 1 + k, t : t + 32, lo:hi] = v.astype(BF16)
                send2(p, g, 4 + k, 1 + k, t, second[g][k])

    def stage_v(p):
        lo, n = PIECES[p]
        hi = lo + n
        val = []
        for g in range(2):
            for i in (2, 3, 4, 5):
                slow[p][g][i].wait_recv()
            val.append(own2[g, :, lo:hi] + r2[g, 1, :, lo:hi].astype(F32) + r2[g, 2, :, lo:hi].astype(F32))
        if hi > COLS:
            lane = lax.broadcasted_iota(jnp.int32, (64, 128), 1)
            tail = val[0][:, n - 128 :] + val[1][:, n - 128 :]
            tot = jnp.sum(jnp.where(lane >= 112, tail, 0.0), axis=1, keepdims=True)
            rscale[...] = jnp.broadcast_to(lax.rsqrt(tot / D + EPSILON), (64, 128))
        scale = rscale[:, :1]
        gate, up = val[0] * scale, val[1] * scale
        hidden = (gate / (1.0 + jnp.exp(-gate)) * up).astype(BF16)
        m = min(n, COLS - lo)
        out_ref[:, lo : lo + m] = hidden[:, :m]

    def stage_cache(p):
        kv_copy[6].wait_recv()
        kv_copy[7].wait_recv()
        group = lax.broadcasted_iota(jnp.int32, (256, 64), 0) // 32
        hit = jnp.where(pages_ref[...] == r * 8 + group, 1.0, 0.0)
        has = jnp.sum(hit, axis=1, keepdims=True) > 0.5
        hit = hit.astype(BF16)
        slot = lax.broadcasted_iota(jnp.int32, (256, 512), 0)
        tok = lax.broadcasted_iota(jnp.int32, (256, 512), 1)
        src = lax.broadcasted_iota(jnp.int32, (64, 512), 0)
        dst = lax.broadcasted_iota(jnp.int32, (64, 512), 1) // 32
        new = jnp.zeros((256, 128), F32)
        for a in range(4):
            spread = jnp.where(src == a * 16 + dst, 1.0, 0.0).astype(BF16)
            pick = jnp.dot(hit, spread, preferred_element_type=F32)
            pick = jnp.where(slot % 32 == tok % 32, pick, 0.0).astype(BF16)
            new += jnp.dot(pick, kvb[a].reshape(512, 128), preferred_element_type=F32)
        old = cache_ref[...].astype(F32)
        cout_ref[...] = jnp.where(has & (new < 0.5 * DEAD), new, old).astype(BF16)

    for stage, p in (
        (stage_x, 0), (stage_x, 1), (stage_y, 0), (stage_x, 2), (stage_y, 1), (stage_z, 0),
        (stage_x, 3), (stage_y, 2), (stage_z, 1), (stage_u, 0), (stage_cache, 0), (stage_y, 3),
        (stage_z, 2), (stage_u, 1), (stage_v, 0), (stage_z, 3), (stage_u, 2), (stage_v, 1),
        (stage_u, 3), (stage_v, 2), (stage_v, 3),
    ):
        stage(p)
    for copy in started:
        copy.wait_send()


def layer(*args):
    vm = pl.BlockSpec(memory_space=pltpu.VMEM)
    hbm = pl.BlockSpec(memory_space=pl.ANY)
    dma = pltpu.SemaphoreType.DMA
    return pl.pallas_call(
        layer_kernel,
        out_shape=(
            jax.ShapeDtypeStruct((64, COLS), BF16),
            jax.ShapeDtypeStruct((256, 128), BF16),
        ),
        in_specs=[vm] * 6 + [hbm] * 3,
        out_specs=(vm, vm),
        scratch_shapes=[
            pltpu.VMEM((4, 4, 64, 512), BF16),
            pltpu.VMEM((1024, 512), BF16),
            pltpu.VMEM((2, 4, 4, 64, 512), BF16),
            pltpu.VMEM((4, 4, 128, 128), BF16),
            pltpu.VMEM((4, 256, 256), F32),
            pltpu.VMEM((4, 256, 256), BF16),
            pltpu.VMEM((4, 256, 256), BF16),
            pltpu.VMEM((4, 3, 64, 256), BF16),
            pltpu.VMEM((4, 3, 64, 256), BF16),
            pltpu.VMEM((4, 64, 256), F32),
            pltpu.VMEM((4, 2, 4, 64, 256), BF16),
            pltpu.VMEM((4, 4, 64, 512), BF16),
            pltpu.VMEM((2, WIDE, 512), BF16),
            pltpu.VMEM((4, 4, 64, 128), F32),
            pltpu.VMEM((2, 4, 64, 1024), F32),
            pltpu.VMEM((2, 64, WIDE), F32),
            pltpu.VMEM((64, 128), F32),
            pltpu.VMEM((2, 3, 4, 64, WIDE), BF16),
            pltpu.VMEM((2, 3, 4, 64, WIDE), BF16),
            pltpu.VMEM((2, 3, 64, WIDE), BF16),
            pltpu.VMEM((2, 3, 64, WIDE), BF16),
            dma((2,)),
            dma((4, 2)),
            dma((2, 5, 4)), dma((2, 5, 4)),
            dma((8,)), dma((8,)),
            dma((4,)), dma((4,)),
            dma((4, 10)), dma((4, 10)),
            dma((4,)), dma((4,)),
            dma((4, 2, 6)), dma((4, 2, 6)),
            dma((4, 2, 6)), dma((4, 2, 6)),
        ],
        compiler_params=pltpu.CompilerParams(collective_id=0, has_side_effects=True, vmem_limit_bytes=67043328),
        name="layer",
    )(*args)


def on_device(
    segments, queries, keys_values, page_table, paged_cache, residual, out_weight, norm_gain, gate_up_weight
):
    hidden, cache = layer(
        segments[None, :], page_table[None, :], norm_gain[None, :], queries, keys_values.reshape(128, 128),
        paged_cache.reshape(256, 128), residual.reshape(4, 4, 64, 512), out_weight,
        gate_up_weight.transpose(1, 2, 0),
    )
    return hidden, cache.reshape(8, 16, 2, 128)


def solution(mesh):
    placed = (
        P("req"),
        P("req", "mdl"),
        P("req", None, "mdl"),
        P(),
        P("req", None, None, "mdl"),
        P(None, "req"),
        P("mdl", "req"),
        P("req"),
        P("req", None, "mdl"),
    )
    return jax.shard_map(
        on_device,
        mesh=mesh,
        in_specs=placed,
        out_specs=(P("req", "mdl"), P("req", None, None, "mdl")),
        check_vma=False,
    )
```

```python
import jax
import jax.numpy as jnp
from jax import lax
from jax.experimental import pallas as pl
from jax.experimental.pallas import tpu as pltpu
from jax.sharding import PartitionSpec as P

D = 8192
HD = 128
QPK = 8
PAGE = 16
EPSILON = 1e-06
MESH = pl.DeviceIdType.MESH
F32 = jnp.float32
BF16 = jnp.bfloat16
DEAD = 512.0
NT = (((1,), (1,)), ((), ()))


def position():
    req, mdl = lax.axis_index("req"), lax.axis_index("mdl")
    return req // 4, req % 4, mdl // 2, mdl % 2


def dev(y, z, x, c):
    return (y * 4 + z, x * 2 + c)


def ring(v, step):
    return lax.rem(v + step + 4, 4)


def barrier(peers):
    sem = pltpu.get_barrier_semaphore()
    for peer in peers:
        pl.semaphore_signal(sem, inc=1, device_id=peer, device_id_type=MESH)
    pl.semaphore_wait(sem, len(peers))


def copy_to(src, dst, ssem, rsem, peer):
    return pltpu.make_async_remote_copy(
        src_ref=src, dst_ref=dst, send_sem=ssem, recv_sem=rsem, device_id=peer, device_id_type=MESH
    )


WIDE = 3712
COLS = 3696
QUART = 384
SHARED = 4 * QUART
PIECES = ((3072, 640), (1536, 768), (2304, 768))
WIDEST = 768
OWNED = WIDE - SHARED


def quarter(q):
    return pl.ds(pl.multiple_of(q * QUART, QUART), QUART)


def layer_kernel(
    seg_ref, pages_ref, gain_ref, q_ref, kv_ref, cache_ref, res_hbm, ow_hbm, w_ref,
    out_ref, cout_ref,
    res_ref, ow_ref, ag, kvb, acc_own, p2s, p2r, s2s, s2r, chunk_own, n2, ng_ref,
    w, ss, own1, own2, rscale, s1, r1, s2, r2,
    wx, wt, nz, sw, rw, ownw, fs, fr, ft,
    in_sem, w_sem, ag_ss, ag_rs, kv_ss, kv_rs, p_ss, p_rs, x_ss, x_rs, n_ss, n_rs,
    ss1, rs1, ss2, rs2,
    own_sem, wa_ss, wa_rs, nz_ss, nz_rs, xz_ss, xz_rs, sw_ss, sw_rs, fa_ss, fa_rs,
):
    y, z, x, c = position()
    zp, zm = dev(y, ring(z, 1), x, c), dev(y, ring(z, -1), x, c)
    yp, ym = dev(ring(y, 1), z, x, c), dev(ring(y, -1), z, x, c)
    xp, xm = dev(y, z, ring(x, 1), c), dev(y, z, ring(x, -1), c)
    partner = dev(y, z, x, 1 - c)
    ow_load = pltpu.make_async_copy(ow_hbm, ow_ref, in_sem.at[0])
    res_load = pltpu.make_async_copy(res_hbm, res_ref, in_sem.at[1])
    ow_load.start()
    res_load.start()
    loads = []
    for p, (lo, n) in enumerate(PIECES):
        for g in range(2):
            m = min(n, COLS - lo)
            loads.append(
                pltpu.make_async_copy(w_ref.at[g, pl.ds(lo, m)], w.at[g, pl.ds(lo - SHARED, m)], w_sem.at[p, g])
            )
            loads[-1].start()
    for g, f in enumerate((z, y)):
        loads.append(pltpu.make_async_copy(w_ref.at[g, quarter(f)], wx.at[g, f], own_sem.at[g]))
        loads[-1].start()
    started = []

    def go(copy):
        copy.start()
        started.append(copy)
        return copy

    seg = jnp.broadcast_to(seg_ref[...].astype(F32), (128, 64))
    wide_row = lax.broadcasted_iota(jnp.int32, (128, 64), 0)
    wide_col = lax.broadcasted_iota(jnp.int32, (128, 64), 1)
    seg_kv = jnp.sum(jnp.where(wide_col == wide_row // 2, seg, 0.0), axis=1, keepdims=True)
    segc = jnp.sum(jnp.where(wide_col == wide_row, seg, 0.0)[:64], axis=1, keepdims=True)
    row = lax.broadcasted_iota(jnp.int32, (64, 128), 0)
    col = lax.broadcasted_iota(jnp.int32, (64, 128), 1)
    segr = jnp.sum(jnp.where(col // 2 == row, segc, 0.0), axis=0, keepdims=True)
    allowed = ((segc == segr) & (segc >= 0) & (col // 2 < row)) | (col // 2 == row)
    allowed = allowed & (col % 2 == 0)
    live = segc >= 0
    kv = kv_ref[...]
    for h in range(QPK):
        s = lax.dot_general(q_ref[:, h * HD : (h + 1) * HD], kv, NT, preferred_element_type=F32)
        s = jnp.where(allowed, s * HD ** (-0.5), -jnp.inf)
        e = jnp.exp(s - jnp.max(s, axis=-1, keepdims=True))
        probs = pltpu.roll(e / jnp.sum(e, axis=-1, keepdims=True), 1, 1).astype(BF16)
        mixed = jnp.dot(probs, kv, preferred_element_type=F32)
        half, at = h // 4, (h % 4) * HD
        ag[half, y, z, :, at : at + HD] = jnp.where(live, mixed, 0.0).astype(BF16)
    kvb[y, z] = jnp.where(seg_kv >= 0, kv.astype(F32), DEAD).astype(BF16)
    barrier((zp, zm, yp, ym, xp, xm, partner))

    first = ((zp, zm), (yp, ym))
    second = ((yp, ym), (zp, zm))
    fc, sc = (z, y), (y, z)

    def block(half, f, s, lo=0, n=64):
        a, b = (s, f) if half == 0 else (f, s)
        return ag.at[half, a, b, pl.ds(lo, n)]

    def ag_copy(half, j, k, ref, peer):
        return copy_to(ref, ref, ag_ss.at[half, j, k], ag_rs.at[half, j, k], peer)

    one = [[None] * 4 for _ in range(2)]
    two = [[[None] * 4 for _ in range(4)] for _ in range(2)]
    offs = (0, -1, 1, 2)

    def start_one(half):
        ref = block(half, fc[half], sc[half])
        for k in range(2):
            one[half][k] = go(ag_copy(half, 4, k, ref, first[half][k]))

    def forward_one(half, k):
        one[half][k].wait_recv()
        ref = block(half, ring(fc[half], -1 if k == 0 else 1), sc[half], 32 * k, 32)
        one[half][2 + k] = go(ag_copy(half, 4, 2 + k, ref, first[half][k]))

    def start_two(half, j):
        ref = block(half, ring(fc[half], offs[j]), sc[half])
        for k in range(2):
            two[half][j][k] = go(ag_copy(half, j, k, ref, second[half][k]))

    def forward_two(half, j):
        for k in range(2):
            two[half][j][k].wait_recv()
            ref = block(half, ring(fc[half], offs[j]), ring(sc[half], -1 if k == 0 else 1), 32 * k, 32)
            two[half][j][2 + k] = go(ag_copy(half, j, 2 + k, ref, second[half][k]))

    def finish_one(half):
        for k in (2, 3):
            one[half][k].wait_recv()

    def finish_two(half, j):
        for k in (2, 3):
            two[half][j][k].wait_recv()

    kv_copy = [None] * 8

    def kv_msg(i, ref, peer):
        kv_copy[i] = go(copy_to(ref, ref, kv_ss.at[i], kv_rs.at[i], peer))

    def kv_start():
        kv_msg(0, kvb.at[y, z], zp)
        kv_msg(1, kvb.at[y, z], zm)

    def kv_forward():
        kv_copy[0].wait_recv()
        kv_msg(2, kvb.at[y, ring(z, -1), pl.ds(0, 64)], zp)
        kv_copy[1].wait_recv()
        kv_msg(3, kvb.at[y, ring(z, 1), pl.ds(64, 64)], zm)

    def kv_rows():
        kv_copy[2].wait_recv()
        kv_copy[3].wait_recv()
        kv_msg(4, kvb.at[y], yp)
        kv_msg(5, kvb.at[y], ym)

    def kv_rows_forward():
        kv_copy[4].wait_recv()
        kv_msg(6, kvb.at[ring(y, -1), pl.ds(0, 2)], yp)
        kv_copy[5].wait_recv()
        kv_msg(7, kvb.at[ring(y, 1), pl.ds(2, 2)], ym)

    p_copy = [None] * 4
    x_copy = [[None] * 10 for _ in range(4)]
    n_copy = [None] * 4
    top, bot = slice(0, 32), slice(32, 64)
    ds_top, ds_bot = pl.ds(0, 32), pl.ds(32, 32)

    def project(g):
        ya = ring(y, offs[g])
        acc = jnp.dot(ag[0, ya].reshape(256, 512), ow_ref[:512], preferred_element_type=F32)
        acc += jnp.dot(ag[1, ya].reshape(256, 512), ow_ref[512:], preferred_element_type=F32)
        low, high = acc[:, :256], acc[:, 256:]
        acc_own[g] = jnp.where(c == 0, low, high)
        p2s[g] = jnp.where(c == 0, high, low).astype(BF16)
        p_copy[g] = go(copy_to(p2s.at[g], p2r.at[g], p_ss.at[g], p_rs.at[g], partner))

    def xmsg(g, i, k, rows, peer):
        x_copy[g][i] = go(copy_to(s2s.at[g, k, rows], s2r.at[g, k, rows], x_ss.at[g, i], x_rs.at[g, i], peer))

    def reduce_a(g):
        p_copy[g].wait_recv()

        def part(xx):
            rows = pl.ds(pl.multiple_of(xx * 64, 64), 64)
            return acc_own[g, rows, :] + p2r[g, rows, :].astype(F32)

        s2s[g, 0] = part(ring(x, 2)).astype(BF16)
        xmsg(g, 0, 0, ds_top, xp)
        xmsg(g, 1, 0, ds_bot, xm)
        s2s[g, 1] = part(ring(x, 1)).astype(BF16)
        xmsg(g, 2, 1, ds_bot, xp)
        s2s[g, 2] = part(ring(x, -1)).astype(BF16)
        xmsg(g, 3, 2, ds_top, xm)
        chunk_own[g] = part(x)

    def reduce_b(g):
        x_copy[g][0].wait_recv()
        s2s[g, 1, top] = (s2s[g, 1, top].astype(F32) + s2r[g, 0, top].astype(F32)).astype(BF16)
        xmsg(g, 4, 1, ds_top, xp)
        x_copy[g][1].wait_recv()
        s2s[g, 2, bot] = (s2s[g, 2, bot].astype(F32) + s2r[g, 0, bot].astype(F32)).astype(BF16)
        xmsg(g, 5, 2, ds_bot, xm)

    def nmsg(g, i, ref, peer):
        x_copy[g][i] = go(copy_to(ref, ref, x_ss.at[g, i], x_rs.at[g, i], peer))

    gain_row = gain_ref[...].astype(F32)
    gain = jnp.where(c == 0, gain_row[:, :256], gain_row[:, 256:])
    ginv = 1.0 / gain_row

    def reduce_c(g):
        ya = ring(y, offs[g])
        for i in (2, 3, 4, 5):
            x_copy[g][i].wait_recv()
        total = chunk_own[g] + s2r[g, 1].astype(F32) + s2r[g, 2].astype(F32)
        res = res_ref[ya, x].astype(F32)
        stream = total + jnp.where(c == 0, res[:, :256], res[:, 256:])
        n2[ya, c, x] = (stream * gain).astype(BF16)
        nmsg(g, 6, n2.at[ya, c, x], xp)
        nmsg(g, 7, n2.at[ya, c, x], xm)

    def reduce_d(g):
        ya = ring(y, offs[g])
        x_copy[g][6].wait_recv()
        nmsg(g, 8, n2.at[ya, c, ring(x, -1), ds_top], xp)
        x_copy[g][7].wait_recv()
        nmsg(g, 9, n2.at[ya, c, ring(x, 1), ds_bot], xm)

    def reduce_e(g):
        ya = ring(y, offs[g])
        x_copy[g][8].wait_recv()
        x_copy[g][9].wait_recv()
        ref = n2.at[ya, c]
        n_copy[g] = go(copy_to(ref, ref, n_ss.at[g], n_rs.at[g], partner))

    def reduce_f(g):
        ya = ring(y, offs[g])
        n_copy[g].wait_recv()
        squares = 0.0
        for h in range(2):
            at = slice(h * 256, h * 256 + 256)
            v = n2[ya, h]
            ng_ref[ya, :, :, at] = v
            v = v.reshape(256, 256).astype(F32) * ginv[:, at]
            squares += jnp.sum(v * v, axis=1, keepdims=True)
        ss[ya] = jnp.broadcast_to(squares, (256, 128)).reshape(4, 64, 128)

    def swap_start(g, src, dst, far, far_dst, ss_, rs_):
        f = fc[g]
        plus, minus = first[g]
        return [
            go(copy_to(src(ring(f, 1)), dst(f), ss_.at[g, 0], rs_.at[g, 0], plus)),
            go(copy_to(src(ring(f, -1)), dst(f), ss_.at[g, 1], rs_.at[g, 1], minus)),
            go(copy_to(far(0), far_dst(0), ss_.at[g, 2], rs_.at[g, 2], plus)),
            go(copy_to(far(1), far_dst(1), ss_.at[g, 3], rs_.at[g, 3], minus)),
        ]

    def swap_relay(g, copies, held, dst, ss_, rs_):
        f = fc[g]
        plus, minus = first[g]
        copies[2].wait_recv()
        copies.append(go(copy_to(held(0), dst(ring(f, -1), 0), ss_.at[g, 4], rs_.at[g, 4], plus)))
        copies[3].wait_recv()
        copies.append(go(copy_to(held(1), dst(ring(f, 1), 1), ss_.at[g, 5], rs_.at[g, 5], minus)))

    def swap_finish(copies):
        for i in (0, 1, 4, 5):
            copies[i].wait_recv()

    weights = [None] * 2
    half_q = QUART // 2

    def weights_start():
        for g in range(2):

            def far(k, g=g):
                at = ring(fc[g], 2) * QUART + k * half_q
                return w_ref.at[g, pl.ds(pl.multiple_of(at, half_q), half_q)]

            weights[g] = swap_start(
                g, lambda q: w_ref.at[g, quarter(q)], lambda p: wx.at[g, p],
                far, lambda k: wt.at[g, k], wa_ss, wa_rs,
            )

    def weights_relay():
        for g in range(2):
            swap_relay(
                g, weights[g], lambda k: wt.at[g, k],
                lambda p, k: wx.at[g, p, pl.ds(k * half_q, half_q)], wa_ss, wa_rs,
            )

    rows_copy = [[None] * 4 for _ in range(2)]
    side = [[[None] * 5 for _ in range(3)] for _ in range(2)]
    every = slice(None)

    def rows_start():
        for g in range(2):
            for k in range(2):
                rows_copy[g][k] = go(copy_to(
                    n2.at[every, c, x], nz.at[g, k, every, c, x], nz_ss.at[g, k], nz_rs.at[g, k], first[g][k]
                ))

    def rows_relay():
        for g in range(2):
            for k in range(2):
                rows_copy[g][k].wait_recv()
                at = pl.ds(2 * k, 2)
                rows_copy[g][2 + k] = go(copy_to(
                    nz.at[g, k, at, c, x], nz.at[g, 2, at, c, x], nz_ss.at[g, 2 + k], nz_rs.at[g, 2 + k], first[g][k]
                ))

    def side_msg(g, j, i, ref, peer):
        side[g][j][i] = go(copy_to(ref, ref, xz_ss.at[g, j, i], xz_rs.at[g, j, i], peer))

    def side_start(j):
        for g in range(2):
            if j == 2:
                rows_copy[g][2].wait_recv()
                rows_copy[g][3].wait_recv()
            side_msg(g, j, 0, nz.at[g, j, every, c, x], xp)
            side_msg(g, j, 1, nz.at[g, j, every, c, x], xm)

    def side_relay(j):
        for g in range(2):
            side[g][j][0].wait_recv()
            side_msg(g, j, 2, nz.at[g, j, pl.ds(0, 2), c, ring(x, -1)], xp)
            side[g][j][1].wait_recv()
            side_msg(g, j, 3, nz.at[g, j, pl.ds(2, 2), c, ring(x, 1)], xm)

    def side_pair(j):
        for g in range(2):
            side[g][j][2].wait_recv()
            side[g][j][3].wait_recv()
            side_msg(g, j, 4, nz.at[g, j, every, c], partner)

    def side_finish(j):
        for g in range(2):
            side[g][j][4].wait_recv()

    for half in range(2):
        start_one(half)
    for half in range(2):
        start_two(half, 0)
    for half in range(2):
        for k in range(2):
            forward_one(half, k)
            start_two(half, 1 + k)
    for half in range(2):
        forward_two(half, 0)
    for half in range(2):
        finish_one(half)
        start_two(half, 3)
    kv_start()
    ow_load.wait()
    finish_two(1, 0)
    project(0)
    for j in (1, 2):
        for half in range(2):
            forward_two(half, j)
    reduce_a(0)
    for half in range(2):
        forward_two(half, 3)
    weights_start()
    finish_two(1, 1)
    project(1)
    reduce_b(0)
    finish_two(1, 2)
    project(2)
    kv_forward()
    reduce_a(1)
    res_load.wait()
    reduce_c(0)
    reduce_a(2)
    reduce_b(1)
    finish_two(1, 3)
    for j in range(4):
        finish_two(0, j)
    project(3)
    kv_rows()
    reduce_d(0)
    reduce_b(2)
    reduce_c(1)
    reduce_a(3)
    reduce_e(0)
    reduce_d(1)
    reduce_c(2)
    reduce_b(3)
    reduce_e(1)
    reduce_f(0)
    reduce_d(2)
    reduce_c(3)
    reduce_e(2)
    reduce_f(1)
    kv_rows_forward()
    rows_start()
    reduce_d(3)
    reduce_f(2)
    reduce_e(3)
    weights_relay()
    reduce_f(3)

    r = lax.axis_index("req")

    def rows_of(ref, g, d, n):
        v = ref[:, pl.ds(d, 1)] if g == 0 else ref[pl.ds(d, 1)]
        return v.reshape(256, n)

    def partial(g, d, p):
        lo, n = PIECES[p]
        at = slice(lo - SHARED, lo - SHARED + n)
        out = lax.dot_general(rows_of(ng_ref, g, d, 512), w[g, at], NT, preferred_element_type=F32)
        if lo + n > COLS:
            tot = rows_of(ss, g, d, 128)
            high = tot.astype(BF16).astype(F32)
            mine = high if g == 0 else tot - high
            lane = lax.broadcasted_iota(jnp.int32, (256, 128), 1)
            tail = out[:, n - 128 :]
            tail = jnp.where(lane < 112, tail, jnp.where(lane == 112 + r, mine, 0.0))
            out = jnp.concatenate([out[:, : n - 128], tail], axis=1)
        return out.reshape(4, 64, n)

    fast = [[[None] * 6 for _ in range(2)] for _ in range(3)]
    slow = [[[None] * 6 for _ in range(2)] for _ in range(3)]

    def send1(p, g, i, k, t, peer):
        lo, n = PIECES[p]
        at = (g, k, pl.ds(t, 2), slice(None), pl.ds(lo - SHARED, n))
        fast[p][g][i] = go(copy_to(s1.at[at], r1.at[at], ss1.at[p, g, i], rs1.at[p, g, i], peer))

    def send2(p, g, i, k, t, peer):
        lo, n = PIECES[p]
        at = (g, k, pl.ds(t, 32), pl.ds(lo - SHARED, n))
        slow[p][g][i] = go(copy_to(s2.at[at], r2.at[at], ss2.at[p, g, i], rs2.at[p, g, i], peer))

    def swiglu(gate, up):
        return (gate / (1.0 + jnp.exp(-gate)) * up).astype(BF16)

    def stage_x(p):
        lo, n = PIECES[p]
        lo -= SHARED
        hi = lo + n
        for g in range(2):
            loads[2 * p + g].wait()
            s1[g, 0, :, :, lo:hi] = partial(g, ring(fc[g], 2), p).astype(BF16)
            send1(p, g, 0, 0, 0, first[g][0])
            send1(p, g, 1, 0, 2, first[g][1])
        for g in range(2):
            s1[g, 1, :, :, lo:hi] = partial(g, ring(fc[g], 1), p).astype(BF16)
            send1(p, g, 2, 1, 2, first[g][0])
            s1[g, 2, :, :, lo:hi] = partial(g, ring(fc[g], -1), p).astype(BF16)
            send1(p, g, 3, 2, 0, first[g][1])

    def stage_y(p):
        lo, n = PIECES[p]
        lo -= SHARED
        hi = lo + n
        for g in range(2):
            for k in range(2):
                t = 2 * k
                fast[p][g][k].wait_recv()
                v = s1[g, 1 + k, t : t + 2, :, lo:hi].astype(F32) + r1[g, 0, t : t + 2, :, lo:hi].astype(F32)
                s1[g, 1 + k, t : t + 2, :, lo:hi] = v.astype(BF16)
                send1(p, g, 4 + k, 1 + k, t, first[g][k])

    def stage_z(p):
        lo, n = PIECES[p]
        lo -= SHARED
        hi = lo + n
        for g in range(2):
            own1[g, :, :, :n] = partial(g, fc[g], p)
        for g in range(2):
            for i in (2, 3, 4, 5):
                fast[p][g][i].wait_recv()

            def summed(t):
                at = (pl.ds(t, 1), slice(None))
                return (
                    own1[g, pl.ds(t, 1), :, :n]
                    + r1[g, 1, pl.ds(t, 1), :, lo:hi].astype(F32)
                    + r1[g, 2, pl.ds(t, 1), :, lo:hi].astype(F32)
                ).reshape(64, n)

            s2[g, 0, :, lo:hi] = summed(ring(sc[g], 2)).astype(BF16)
            send2(p, g, 0, 0, 0, second[g][0])
            send2(p, g, 1, 0, 32, second[g][1])
            s2[g, 1, :, lo:hi] = summed(ring(sc[g], 1)).astype(BF16)
            send2(p, g, 2, 1, 32, second[g][0])
            s2[g, 2, :, lo:hi] = summed(ring(sc[g], -1)).astype(BF16)
            send2(p, g, 3, 2, 0, second[g][1])
            own2[g, :, lo:hi] = summed(sc[g])

    def stage_u(p):
        lo, n = PIECES[p]
        lo -= SHARED
        hi = lo + n
        for g in range(2):
            for k in range(2):
                t = 32 * k
                slow[p][g][k].wait_recv()
                v = s2[g, 1 + k, t : t + 32, lo:hi].astype(F32) + r2[g, 0, t : t + 32, lo:hi].astype(F32)
                s2[g, 1 + k, t : t + 32, lo:hi] = v.astype(BF16)
                send2(p, g, 4 + k, 1 + k, t, second[g][k])

    def stage_v(p):
        lo, n = PIECES[p]
        lo -= SHARED
        hi = lo + n
        val = []
        for g in range(2):
            for i in (2, 3, 4, 5):
                slow[p][g][i].wait_recv()
            val.append(own2[g, :, lo:hi] + r2[g, 1, :, lo:hi].astype(F32) + r2[g, 2, :, lo:hi].astype(F32))
        if hi > COLS - SHARED:
            lane = lax.broadcasted_iota(jnp.int32, (64, 128), 1)
            tail = val[0][:, n - 128 :] + val[1][:, n - 128 :]
            tot = jnp.sum(jnp.where(lane >= 112, tail, 0.0), axis=1, keepdims=True)
            rscale[...] = jnp.broadcast_to(lax.rsqrt(tot / D + EPSILON), (64, 128))
        scale = rscale[:, :1]
        hidden = swiglu(val[0] * scale, val[1] * scale)
        m = min(n, COLS - SHARED - lo)
        out_ref[:, SHARED + lo : SHARED + lo + m] = hidden[:, :m]

    ring_w = [[None] * 6 for _ in range(2)]
    back_w = [None] * 2

    def shared_partial(g, d):
        out = 0.0
        for j, off in ((None, 0), (0, -1), (1, 1), (2, 2)):
            p = ring(fc[g], off)
            for h in range(2):
                if g == 0:
                    v = n2[pl.ds(d, 1), h] if j is None else nz[g, j, pl.ds(d, 1), h]
                else:
                    v = n2[:, h, pl.ds(d, 1)] if j is None else nz[g, j, :, h, pl.ds(d, 1)]
                u = wx[g, pl.ds(p, 1), :, h * 256 : h * 256 + 256].reshape(QUART, 256)
                out += lax.dot_general(v.reshape(256, 256), u, NT, preferred_element_type=F32)
        return out.reshape(4, 64, QUART)

    def send_w(g, i, k, t, peer):
        at = (g, k, pl.ds(t, 2))
        ring_w[g][i] = go(copy_to(sw.at[at], rw.at[at], sw_ss.at[g, i], sw_rs.at[g, i], peer))

    def shared_x(p):
        for g in range(2):
            swap_finish(weights[g])
            loads[2 * len(PIECES) + g].wait()
            sw[g, 0] = shared_partial(g, ring(sc[g], 2)).astype(BF16)
            send_w(g, 0, 0, 0, second[g][0])
            send_w(g, 1, 0, 2, second[g][1])
        for g in range(2):
            sw[g, 1] = shared_partial(g, ring(sc[g], 1)).astype(BF16)
            send_w(g, 2, 1, 2, second[g][0])
            sw[g, 2] = shared_partial(g, ring(sc[g], -1)).astype(BF16)
            send_w(g, 3, 2, 0, second[g][1])

    def shared_y(p):
        for g in range(2):
            for k in range(2):
                t = 2 * k
                ring_w[g][k].wait_recv()
                v = sw[g, 1 + k, t : t + 2].astype(F32) + rw[g, 0, t : t + 2].astype(F32)
                sw[g, 1 + k, t : t + 2] = v.astype(BF16)
                send_w(g, 4 + k, 1 + k, t, second[g][k])

    def shared_own(p):
        for g in range(2):
            ownw[g] = shared_partial(g, sc[g])

    def shared_z(p):
        for g in range(2):
            for i in (2, 3, 4, 5):
                ring_w[g][i].wait_recv()
            fs[g] = (ownw[g] + rw[g, 1].astype(F32) + rw[g, 2].astype(F32)).astype(BF16)
            fr[g, pl.ds(fc[g], 1)] = fs[g, pl.ds(fc[g], 1)]
            back_w[g] = swap_start(
                g, lambda q: fs.at[g, q], lambda q: fr.at[g, q],
                lambda k: fs.at[g, ring(fc[g], 2), pl.ds(32 * k, 32)], lambda k: ft.at[g, k], fa_ss, fa_rs,
            )

    def shared_u(p):
        for g in range(2):
            swap_relay(
                g, back_w[g], lambda k: ft.at[g, k],
                lambda q, k: fr.at[g, q, pl.ds(32 * k, 32)], fa_ss, fa_rs,
            )

    def shared_v(p):
        for g in range(2):
            swap_finish(back_w[g])
        scale = rscale[:, :1]
        for q in range(4):
            out_ref[:, q * QUART : (q + 1) * QUART] = swiglu(
                fr[0, q].astype(F32) * scale, fr[1, q].astype(F32) * scale
            )

    def stage_cache(p):
        kv_copy[6].wait_recv()
        kv_copy[7].wait_recv()
        group = lax.broadcasted_iota(jnp.int32, (256, 64), 0) // 32
        hit = jnp.where(pages_ref[...] == r * 8 + group, 1.0, 0.0)
        has = jnp.sum(hit, axis=1, keepdims=True) > 0.5
        hit = hit.astype(BF16)
        slot = lax.broadcasted_iota(jnp.int32, (256, 512), 0)
        tok = lax.broadcasted_iota(jnp.int32, (256, 512), 1)
        src = lax.broadcasted_iota(jnp.int32, (64, 512), 0)
        dst = lax.broadcasted_iota(jnp.int32, (64, 512), 1) // 32
        new = jnp.zeros((256, 128), F32)
        for a in range(4):
            spread = jnp.where(src == a * 16 + dst, 1.0, 0.0).astype(BF16)
            pick = jnp.dot(hit, spread, preferred_element_type=F32)
            pick = jnp.where(slot % 32 == tok % 32, pick, 0.0).astype(BF16)
            new += jnp.dot(pick, kvb[a].reshape(512, 128), preferred_element_type=F32)
        old = cache_ref[...].astype(F32)
        cout_ref[...] = jnp.where(has & (new < 0.5 * DEAD), new, old).astype(BF16)

    def rows_on(p):
        if p < 3:
            side_start(p)
        elif p < 6:
            side_relay(p - 3)
        elif p < 9:
            side_pair(p - 6)
        elif p < 12:
            side_finish(p - 9)
        else:
            rows_relay()

    for stage, p in (
        (stage_x, 0), (rows_on, 12), (rows_on, 0), (rows_on, 1), (stage_x, 1), (stage_y, 0),
        (rows_on, 2), (rows_on, 3), (stage_x, 2), (rows_on, 4), (stage_y, 1), (stage_z, 0),
        (rows_on, 5), (rows_on, 6), (rows_on, 7), (stage_y, 2), (stage_z, 1), (rows_on, 8),
        (rows_on, 9), (rows_on, 10), (stage_u, 0), (rows_on, 11), (shared_x, 0), (stage_u, 1),
        (stage_z, 2), (stage_v, 0), (shared_y, 0), (stage_cache, 0), (shared_own, 0), (stage_u, 2),
        (stage_v, 1), (shared_z, 0), (stage_v, 2), (shared_u, 0), (shared_v, 0),
    ):
        stage(p)
    for copy in started:
        copy.wait_send()


def layer(*args):
    vm = pl.BlockSpec(memory_space=pltpu.VMEM)
    hbm = pl.BlockSpec(memory_space=pl.ANY)
    dma = pltpu.SemaphoreType.DMA
    return pl.pallas_call(
        layer_kernel,
        out_shape=(
            jax.ShapeDtypeStruct((64, COLS), BF16),
            jax.ShapeDtypeStruct((256, 128), BF16),
        ),
        in_specs=[vm] * 6 + [hbm] * 3,
        out_specs=(vm, vm),
        scratch_shapes=[
            pltpu.VMEM((4, 4, 64, 512), BF16),
            pltpu.VMEM((1024, 512), BF16),
            pltpu.VMEM((2, 4, 4, 64, 512), BF16),
            pltpu.VMEM((4, 4, 128, 128), BF16),
            pltpu.VMEM((4, 256, 256), F32),
            pltpu.VMEM((4, 256, 256), BF16),
            pltpu.VMEM((4, 256, 256), BF16),
            pltpu.VMEM((4, 3, 64, 256), BF16),
            pltpu.VMEM((4, 3, 64, 256), BF16),
            pltpu.VMEM((4, 64, 256), F32),
            pltpu.VMEM((4, 2, 4, 64, 256), BF16),
            pltpu.VMEM((4, 4, 64, 512), BF16),
            pltpu.VMEM((2, OWNED, 512), BF16),
            pltpu.VMEM((4, 4, 64, 128), F32),
            pltpu.VMEM((2, 4, 64, WIDEST), F32),
            pltpu.VMEM((2, 64, OWNED), F32),
            pltpu.VMEM((64, 128), F32),
            pltpu.VMEM((2, 3, 4, 64, OWNED), BF16),
            pltpu.VMEM((2, 3, 4, 64, OWNED), BF16),
            pltpu.VMEM((2, 3, 64, OWNED), BF16),
            pltpu.VMEM((2, 3, 64, OWNED), BF16),
            pltpu.VMEM((2, 4, QUART, 512), BF16),
            pltpu.VMEM((2, 2, QUART // 2, 512), BF16),
            pltpu.VMEM((2, 3, 4, 2, 4, 64, 256), BF16),
            pltpu.VMEM((2, 3, 4, 64, QUART), BF16),
            pltpu.VMEM((2, 3, 4, 64, QUART), BF16),
            pltpu.VMEM((2, 4, 64, QUART), F32),
            pltpu.VMEM((2, 4, 64, QUART), BF16),
            pltpu.VMEM((2, 4, 64, QUART), BF16),
            pltpu.VMEM((2, 2, 32, QUART), BF16),
            dma((2,)),
            dma((3, 2)),
            dma((2, 5, 4)), dma((2, 5, 4)),
            dma((8,)), dma((8,)),
            dma((4,)), dma((4,)),
            dma((4, 10)), dma((4, 10)),
            dma((4,)), dma((4,)),
            dma((3, 2, 6)), dma((3, 2, 6)),
            dma((3, 2, 6)), dma((3, 2, 6)),
            dma((2,)),
            dma((2, 6)), dma((2, 6)),
            dma((2, 4)), dma((2, 4)),
            dma((2, 3, 5)), dma((2, 3, 5)),
            dma((2, 6)), dma((2, 6)),
            dma((2, 6)), dma((2, 6)),
        ],
        compiler_params=pltpu.CompilerParams(collective_id=0, has_side_effects=True, vmem_limit_bytes=67043328),
        name="layer",
    )(*args)


def on_device(
    segments, queries, keys_values, page_table, paged_cache, residual, out_weight, norm_gain, gate_up_weight
):
    hidden, cache = layer(
        segments[None, :], page_table[None, :], norm_gain[None, :], queries, keys_values.reshape(128, 128),
        paged_cache.reshape(256, 128), residual.reshape(4, 4, 64, 512), out_weight,
        gate_up_weight.transpose(1, 2, 0),
    )
    return hidden, cache.reshape(8, 16, 2, 128)


def solution(mesh):
    placed = (
        P("req"),
        P("req", "mdl"),
        P("req", None, "mdl"),
        P(),
        P("req", None, None, "mdl"),
        P(None, "req"),
        P("mdl", "req"),
        P("req"),
        P("req", None, "mdl"),
    )
    return jax.shard_map(
        on_device,
        mesh=mesh,
        in_specs=placed,
        out_specs=(P("req", "mdl"), P("req", None, None, "mdl")),
        check_vma=False,
    )
```
